32 devices in a mesh: ty: 4 (over x, core), tx: 8 (over z, y).
Axes of the slice: x: 2, y: 2, z: 4, core: 2. Of those that a mesh axis runs over, the one named last changes fastest.
Arguments:
- stamps: bfloat16 [4, 8, 5, 64, 1024], P('ty', 'tx'), may hold values from 0 to 0.059814453
- positions: int32 [4, 8, 2, 64], P('ty', 'tx'), may hold values from 0 to 1791, as said below
- weights: float32 [5, 256, 1792], P(None, 'ty', 'tx'), may hold values from 0.1 to 1
- mask: int32 [5, 256, 1792], P(None, 'ty', 'tx'), may hold values 0 or 1
- residual: float32 [5, 256, 1792], P(None, 'ty', 'tx'), may hold values from -6 to 6
Outputs:
- gram: float32 [4, 8, 5, 64, 576], P('ty', 'tx')
- rhs: float32 [4, 8, 5, 64], P('ty', 'tx')
The draws below stay inside these ranges and needn't reach their ends.
Inputs may be any that keep to these rules, and one draw needn't show every extreme that they name: Star s of tile (a, c) lies in that tile: positions[a, c, 0, s] is in [a * 64, (a + 1) * 64) and positions[a, c, 1, s] is in [c * 224, (c + 1) * 224).
All inputs are finite; a program needn't handle non-finite values. No bound on the sum of `mask` on one device may be relied on, other than what follows from the above.
Results may differ from the reference program's by a relative error of at most 0.0029.
Values may be sent and summed in bfloat16 or wider, within the bound.
A program may use at most 128 MiB of HBM per device.

```python
import math
import jax
import jax.numpy as jnp
from jax import lax

BANDS = 5
STAMP = 32
STARS = 64
TR = 64
TC = 224
NY = 256
NX = 1792
N_TY = 4
N_TX = 8


def draw_positions(key, part):
    key_rows = jax.random.fold_in(key, 11)
    key_cols = jax.random.fold_in(key, 12)
    row_offsets = jax.random.randint(key_rows, (N_TY, N_TX, STARS), 0, TR, dtype=jnp.int32)
    col_offsets = jax.random.randint(key_cols, (N_TY, N_TX, STARS), 0, TC, dtype=jnp.int32)
    rows_whole = row_offsets + (jnp.arange(N_TY, dtype=jnp.int32) * TR)[:, None, None]
    cols_whole = col_offsets + (jnp.arange(N_TX, dtype=jnp.int32) * TC)[None, :, None]
    return jnp.stack((rows_whole, cols_whole), axis=2).astype(jnp.int32)


def place_ends(array, stream_key, low, top_value):
    spot = [jax.random.randint(jax.random.fold_in(stream_key, axis), (), 0, length) for axis, length in enumerate(array.shape)]
    widest = array.shape.index(max(array.shape))
    next_to = spot[:widest] + [(spot[widest] + 1) % array.shape[widest]] + spot[widest + 1:]
    return array.at[tuple(spot)].set(low).at[tuple(next_to)].set(top_value)


def block_levels(stream_key, shape, split, low, top_value):
    def one(dim, parts):
        steps = jax.random.uniform(jax.random.fold_in(jax.random.fold_in(stream_key, 6), dim), (parts,), jnp.float32, low / len(split), top_value / len(split))
        return jnp.repeat(jnp.exp(steps), shape[dim] // parts).reshape((-1,) + (1,) * (len(shape) - dim - 1))

    level = one(*split[0])
    for cut in split[1:]:
        level = level * one(*cut)
    return level


def gaussian(own_key, dims, scale, bound, pieces=(), held_as=jnp.bfloat16):
    result = jax.random.normal(own_key, dims, jnp.float32) * scale
    if len(pieces) > 0:
        result = block_levels(own_key, dims, pieces, -0.22, 0.18) * result
    return jnp.clip(result, min=-bound, max=bound).astype(held_as)


def setup_inputs(seed: int = 0) -> dict:
    arg_keys = jax.random.split(jax.random.key(seed), 6)
    return {
        "stamps": jnp.clip(0.059814453 * jax.random.uniform(arg_keys[0], (N_TY, N_TX, BANDS, STARS, STAMP * STAMP), jnp.float32) ** block_levels(arg_keys[0], (N_TY, N_TX, BANDS, STARS, STAMP * STAMP), ((0, 4), (1, 8)), -0.2, 0.2), 0.0, 0.059814453).astype(jnp.bfloat16),
        "positions": draw_positions(jax.random.fold_in(arg_keys[5], 71), 0),
        "weights": jnp.clip(jnp.exp(math.log(1.0) - 2.3025851 * jax.random.uniform(arg_keys[2], (BANDS, NY, NX), jnp.float32) ** block_levels(arg_keys[2], (BANDS, NY, NX), ((1, 4), (2, 8)), -0.2, 0.2)), 0.1, 1.0),
        "mask": place_ends((jax.random.randint(arg_keys[3], (BANDS, NY, NX), 0, 10) < 9).astype(jnp.int32), jax.random.fold_in(arg_keys[3], 1), 0, 1),
        "residual": gaussian(arg_keys[4], (BANDS, NY, NX), 1.0, 6.0, ((1, 4), (2, 8)), jnp.float32),
    }


def render_stars(stamp_rows, places, anchor_row, anchor_col, rows_out, cols_out):
    star_count = stamp_rows.shape[0]
    stamp_grid = stamp_rows.astype(jnp.float32).reshape(star_count, STAMP, STAMP)
    start_row = places[0] - anchor_row
    start_col = places[1] - anchor_col
    shape_cols = (star_count, STAMP, cols_out)
    col_pick = (lax.broadcasted_iota(jnp.int32, shape_cols, 2) - lax.broadcasted_iota(jnp.int32, shape_cols, 1) == start_col[:, None, None]).astype(jnp.float32)
    shape_rows = (star_count, STAMP, rows_out)
    row_pick = (lax.broadcasted_iota(jnp.int32, shape_rows, 2) - lax.broadcasted_iota(jnp.int32, shape_rows, 1) == start_row[:, None, None]).astype(jnp.float32)
    placed = jnp.einsum('sij,sjx->six', stamp_grid, col_pick, precision=lax.Precision.HIGHEST)
    picture = jnp.einsum('six,siy->syx', placed, row_pick, precision=lax.Precision.HIGHEST)
    return picture.reshape(star_count, rows_out * cols_out)

def reference(stamps, positions, weights, mask, residual):
    half_side = STAMP // 2
    rows_out = TR + STAMP
    cols_out = TC + STAMP
    weight = weights * mask.astype(jnp.float32)
    spread = ((0, 0), (half_side, half_side), (half_side, half_side))
    root_pad = jnp.pad(jnp.sqrt(weight), spread)
    resid_pad = jnp.pad(weight * residual, spread).astype(jnp.bfloat16)
    stamps_pad = jnp.pad(stamps, ((1, 1), (1, 1), (0, 0), (0, 0), (0, 0)))
    places_pad = jnp.pad(positions, ((1, 1), (1, 1), (0, 0), (0, 0)))

    def tile_terms(tile_index):
        tile_row = tile_index // N_TX
        tile_col = tile_index % N_TX
        anchor_row = tile_row * TR
        anchor_col = tile_col * TC
        zero_start = jnp.zeros((), jnp.int32)
        root_here = lax.dynamic_slice(root_pad, (zero_start, anchor_row, anchor_col), (BANDS, rows_out, cols_out))
        resid_here = lax.dynamic_slice(resid_pad, (zero_start, anchor_row, anchor_col), (BANDS, rows_out, cols_out))
        near_stamps = lax.dynamic_slice(stamps_pad, (tile_row, tile_col, zero_start, zero_start, zero_start), (3, 3, BANDS, STARS, STAMP * STAMP))
        near_places = lax.dynamic_slice(places_pad, (tile_row, tile_col, zero_start, zero_start), (3, 3, 2, STARS))

        def band_terms(band_index):
            root_flat = root_here[band_index].reshape(-1)
            resid_flat = resid_here[band_index].reshape(-1).astype(jnp.float32)
            pictures = [render_stars(near_stamps[offset // 3, offset % 3, band_index], near_places[offset // 3, offset % 3], anchor_row, anchor_col, rows_out, cols_out) for offset in range(9)]
            weighted = [(picture * root_flat[None, :]).astype(jnp.bfloat16) for picture in pictures]
            own_weighted = weighted[4].astype(jnp.float32)
            blocks = [jnp.dot(own_weighted, near_item.astype(jnp.float32).T, precision=lax.Precision.HIGHEST) for near_item in weighted]
            rhs_band = jnp.dot(pictures[4], resid_flat, precision=lax.Precision.HIGHEST)
            return (jnp.concatenate(blocks, axis=1), rhs_band)
        return lax.map(band_terms, jnp.arange(BANDS, dtype=jnp.int32))
    gram, rhs = lax.map(tile_terms, jnp.arange(N_TY * N_TX, dtype=jnp.int32))
    return (gram.reshape(N_TY, N_TX, BANDS, STARS, 9 * STARS), rhs.reshape(N_TY, N_TX, BANDS, STARS))
```

```python
import jax
import jax.numpy as jnp
from jax import lax
from jax.experimental import pallas as pl
from jax.experimental.pallas import tpu as pltpu
from jax.sharding import PartitionSpec as P

STAMP = 32
LANES = 128
GROUP = 8


def padded(cells, sides, width):
    for axis, dim in sides:
        count = lax.axis_size(axis)
        ends = count - 1
        head = lax.slice_in_dim(cells, 0, width, axis=dim)
        tail = lax.slice_in_dim(cells, cells.shape[dim] - width, cells.shape[dim], axis=dim)
        cells = jnp.concatenate(
            [
                lax.ppermute(tail, axis, [(i, i + 1) for i in range(ends)]),
                cells,
                lax.ppermute(head, axis, [(i + 1, i) for i in range(ends)]),
            ],
            axis=dim,
        )
    return cells


def shifted(x, axis, by):
    length = lax.axis_size(axis)
    pairs = [(i, i + by) for i in range(length) if 0 <= i + by < length]
    return lax.ppermute(x, axis, pairs)


def nt_dot(left, right):
    return lax.dot_general(left, right, (((1,), (1,)), ((), ())), preferred_element_type=jnp.float32)


def gram_kernel(
    starts, own_st, right_st, below_st, diag_st, root, resid,
    gram, rhs,
    rows_t, own_lo, own_hi, right_hi, below_lo, below_hi, diag_hi, acc_top, acc_lo, acc_hi,
    *, stars, tile_rows, tile_cols,
):
    edge_lane = tile_cols - LANES

    @pl.when(pl.program_id(0) == 0)
    def _():
        for ref in (own_lo, own_hi, right_hi, below_lo, below_hi, diag_hi):
            @pl.loop(0, ref.shape[0] // 512)
            def _(i):
                ref[pl.ds(pl.multiple_of(i * 512, 512), 512), :] = jnp.zeros((512, LANES), jnp.float32)

    lane = lax.broadcasted_iota(jnp.int32, (stars, LANES), 1)
    lane32 = lax.broadcasted_iota(jnp.int32, (STAMP, LANES), 1)
    per_tile = LANES // STAMP

    for index, (stamp_ref, lo, hi) in enumerate(
        ((own_st, own_lo, own_hi), (right_st, None, right_hi), (below_st, below_lo, below_hi), (diag_st, None, diag_hi))
    ):
        for k in range(STAMP // per_tile):
            x = stamp_ref[0, :, k * LANES:(k + 1) * LANES].astype(jnp.float32)
            for j in range(per_tile):
                moved = x if j == 0 else pltpu.roll(x, LANES - STAMP * j, axis=1)
                row = k * per_tile + j
                rows_t[row * stars:(row + 1) * stars, :] = jnp.where(lane < STAMP, moved, 0.0)

        @pl.loop(0, stars // 8)
        def _(step):
            for u in range(8):
                s = step * 8 + u
                row = starts[index, 0, s]
                col = starts[index, 1, s]
                x = rows_t[pl.ds(s, STAMP, stride=stars), :]
                y = pltpu.roll(x, lax.rem(col, LANES), axis=1)
                spot = pl.ds(row * stars + s, STAMP, stride=stars)
                if lo is None:
                    hi[spot, :] = y
                else:
                    in_lo = lane32 >= col
                    lo[spot, :] = jnp.where(in_lo, y, 0.0)
                    hi[spot, :] = jnp.where(in_lo, 0.0, y)

    acc_top[...] = jnp.zeros_like(acc_top)
    acc_lo[...] = jnp.zeros_like(acc_lo)
    acc_hi[...] = jnp.zeros_like(acc_hi)
    row_lane = lax.broadcasted_iota(jnp.int32, (1, LANES), 1)

    def weigh(ref, y, factor):
        return (ref[pl.ds(pl.multiple_of(y * stars, stars), stars), :] * factor).astype(jnp.bfloat16)

    def group(first, rhs_sum, bottom):
        parts = {name: [] for name in ("ol", "oh", "rh", "bl", "bh", "dh")}
        some = pl.ds(pl.multiple_of(first, GROUP), GROUP)
        root_some, resid_some = root[0, some, :], resid[0, some, :]
        for u in range(GROUP):
            y = first + u
            root_lo = root_some[u:u + 1, :LANES]
            root_hi = root_some[u:u + 1, LANES:]
            root_edge = jnp.where(row_lane >= edge_lane, root_hi, 0.0)
            at = pl.ds(pl.multiple_of(y * stars, stars), stars)
            p_lo = own_lo[at, :]
            p_hi = own_hi[at, :]
            rhs_sum = rhs_sum + p_lo * resid_some[u:u + 1, :LANES] + p_hi * resid_some[u:u + 1, LANES:]
            parts["ol"].append((p_lo * root_lo).astype(jnp.bfloat16))
            parts["oh"].append((p_hi * root_hi).astype(jnp.bfloat16))
            parts["rh"].append(weigh(right_hi, y, root_edge))
            if bottom:
                parts["bl"].append(weigh(below_lo, y - tile_rows, root_lo))
                parts["bh"].append(weigh(below_hi, y - tile_rows, root_hi))
                parts["dh"].append(weigh(diag_hi, y - tile_rows, root_edge))
        q = {name: jnp.concatenate(tiles, axis=1) for name, tiles in parts.items() if tiles}
        if bottom:
            acc_lo[...] += nt_dot(q["ol"], jnp.concatenate([q["ol"], q["bl"]], axis=0))
            four = jnp.concatenate([q["oh"], q["rh"], q["bh"], q["dh"]], axis=0)
            acc_hi[...] += nt_dot(four[:2 * stars], four)
        else:
            acc_top[...] += nt_dot(q["oh"], jnp.concatenate([q["oh"], q["rh"]], axis=0))
            acc_lo[:, :stars] += nt_dot(q["ol"], q["ol"])
        return rhs_sum

    rhs_sum = jnp.zeros((stars, LANES), jnp.float32)
    rhs_sum = lax.fori_loop(0, tile_rows // GROUP, lambda g, r: group(g * GROUP, r, False), rhs_sum)
    rhs_sum = lax.fori_loop(
        0, STAMP // GROUP, lambda g, r: group(tile_rows + g * GROUP, r, True), rhs_sum
    )
    rhs[0] = jnp.sum(rhs_sum, axis=1, keepdims=True)
    n = stars
    top, low, high = acc_top[...], acc_lo[...], acc_hi[...]
    gram[0, 0] = low[:, :n] + top[:, :n] + high[:n, :n]
    gram[0, 1] = top[:, n:2 * n] + high[:n, n:2 * n]
    gram[0, 2] = low[:, n:2 * n] + high[:n, 2 * n:3 * n]
    gram[0, 3] = high[:n, 3 * n:]
    gram[0, 4] = high[n:, 2 * n:3 * n]


def compute(starts, stamp_sets, root, resid, tile_rows, tile_cols):
    bands, stars, pixels = stamp_sets[0].shape
    rows_out, cols_out = root.shape[1:]
    stamp_spec = pl.BlockSpec((1, stars, pixels), lambda b, st: (b, 0, 0))
    field_spec = pl.BlockSpec((1, rows_out, cols_out), lambda b, st: (b, 0, 0))
    tall = pltpu.VMEM((rows_out * stars, LANES), jnp.float32)
    short = pltpu.VMEM((2 * STAMP * stars, LANES), jnp.float32)

    def kernel(*refs):
        gram_kernel(*refs, stars=stars, tile_rows=tile_rows, tile_cols=tile_cols)

    return pl.pallas_call(
        kernel,
        out_shape=(
            jax.ShapeDtypeStruct((bands, 5, stars, stars), jnp.float32),
            jax.ShapeDtypeStruct((bands, stars, 1), jnp.float32),
        ),
        grid_spec=pltpu.PrefetchScalarGridSpec(
            num_scalar_prefetch=1,
            grid=(bands,),
            in_specs=[stamp_spec] * 4 + [field_spec] * 2,
            out_specs=(
                pl.BlockSpec((1, 5, stars, stars), lambda b, st: (b, 0, 0, 0)),
                pl.BlockSpec((1, stars, 1), lambda b, st: (b, 0, 0)),
            ),
            scratch_shapes=[
                pltpu.VMEM((STAMP * stars, LANES), jnp.float32),
                tall, tall, tall, short, short, short,
                pltpu.VMEM((stars, 2 * stars), jnp.float32),
                pltpu.VMEM((stars, 2 * stars), jnp.float32),
                pltpu.VMEM((2 * stars, 4 * stars), jnp.float32),
            ],
        ),
        compiler_params=pltpu.CompilerParams(vmem_limit_bytes=40 << 20),
        name="gram",
    )(starts, *stamp_sets, root, resid)


def body(stamps, positions, weights, mask, residual):
    band_count, tile_rows, tile_cols = weights.shape
    star_count = stamps.shape[3]
    half_side = STAMP // 2
    rows_out = tile_rows + STAMP
    cols_out = tile_cols + STAMP
    own, places = stamps[0, 0], positions[0, 0]
    right = shifted((own, places), "tx", -1)
    below, diag = shifted(((own, places), right), "ty", -1)

    weight = weights * mask.astype(jnp.float32)
    fields = jnp.stack((jnp.sqrt(weight), weight * residual)).astype(jnp.bfloat16)
    region = padded(fields, (("ty", 2), ("tx", 3)), half_side).astype(jnp.float32)

    anchor_row = lax.axis_index("ty") * tile_rows
    anchor_col = lax.axis_index("tx") * tile_cols

    def rows_of(pair):
        return pair[1][0] - anchor_row

    def cols_of(pair):
        return pair[1][1] - anchor_col

    mine = (own, places)
    starts = jnp.stack([
        jnp.stack([jnp.clip(rows_of(mine), 0, tile_rows), jnp.clip(cols_of(mine), 0, tile_cols)]),
        jnp.stack([jnp.clip(rows_of(right), 0, tile_rows), jnp.clip(cols_of(right), tile_cols, cols_out)]),
        jnp.stack([jnp.clip(rows_of(below) - tile_rows, 0, STAMP), jnp.clip(cols_of(below), 0, tile_cols)]),
        jnp.stack([jnp.clip(rows_of(diag) - tile_rows, 0, STAMP), jnp.clip(cols_of(diag), tile_cols, cols_out)]),
    ])
    blocks, rhs = compute(
        starts, (own, right[0], below[0], diag[0]), region[0], region[1], tile_rows, tile_cols
    )
    self_own, own_right, own_below, own_diag, right_below = [blocks[:, i] for i in range(5)]
    to_right = jnp.stack(
        [jnp.swapaxes(own_right, 1, 2), right_below, jnp.swapaxes(own_diag, 1, 2)]
    ).astype(jnp.bfloat16)
    from_left = shifted(to_right, "tx", 1)
    to_below = jnp.stack([jnp.swapaxes(own_below, 1, 2), jnp.swapaxes(right_below, 1, 2)])
    from_above, corner = shifted((to_below, from_left[2]), "ty", 1)
    from_left = from_left.astype(jnp.float32)
    gram = jnp.concatenate(
        [
            corner.astype(jnp.float32), from_above[0], from_above[1],
            from_left[0], self_own, own_right,
            from_left[1], own_below, own_diag,
        ],
        axis=2,
    )
    return (
        gram.reshape(1, 1, band_count, star_count, 9 * star_count),
        rhs.reshape(1, 1, band_count, star_count),
    )


def solution(mesh):
    return jax.shard_map(
        body,
        mesh=mesh,
        in_specs=(
            P("ty", "tx", None, None, None),
            P("ty", "tx", None, None),
            P(None, "ty", "tx"),
            P(None, "ty", "tx"),
            P(None, "ty", "tx"),
        ),
        out_specs=(P("ty", "tx", None, None, None), P("ty", "tx", None, None)),
        check_vma=False,
    )
```

```python
import jax
import jax.numpy as jnp
from jax import lax
from jax.experimental import pallas as pl
from jax.experimental.pallas import tpu as pltpu
from jax.sharding import PartitionSpec as P

STAMP = 32
LANES = 128
GROUP = 8
UNROLL = 16


def padded(cells, sides, width):
    for axis, dim in sides:
        count = lax.axis_size(axis)
        ends = count - 1
        head = lax.slice_in_dim(cells, 0, width, axis=dim)
        tail = lax.slice_in_dim(cells, cells.shape[dim] - width, cells.shape[dim], axis=dim)
        cells = jnp.concatenate(
            [
                lax.ppermute(tail, axis, [(i, i + 1) for i in range(ends)]),
                cells,
                lax.ppermute(head, axis, [(i + 1, i) for i in range(ends)]),
            ],
            axis=dim,
        )
    return cells


def shifted(x, axis, by):
    length = lax.axis_size(axis)
    pairs = [(i, i + by) for i in range(length) if 0 <= i + by < length]
    return lax.ppermute(x, axis, pairs)


def nt_dot(left, right):
    return lax.dot_general(left, right, (((1,), (1,)), ((), ())), preferred_element_type=jnp.float32)


def clear(refs):
    @pl.when(pl.program_id(0) == 0)
    def _():
        for ref in refs:
            @pl.loop(0, ref.shape[0] // 512)
            def _(i):
                ref[pl.ds(pl.multiple_of(i * 512, 512), 512), :] = jnp.zeros((512, LANES), jnp.float32)


def render(spots, shifts, cols, index, stamp_ref, rows_t, lo, hi, stars):
    lane = lax.broadcasted_iota(jnp.int32, (stars, LANES), 1)
    lane32 = lax.broadcasted_iota(jnp.int32, (STAMP, LANES), 1)
    per_tile = LANES // STAMP
    for k in range(STAMP // per_tile):
        x = stamp_ref[0, :, k * LANES:(k + 1) * LANES].astype(jnp.float32)
        for j in range(per_tile):
            moved = x if j == 0 else pltpu.roll(x, LANES - STAMP * j, axis=1)
            row = k * per_tile + j
            rows_t[row * stars:(row + 1) * stars, :] = jnp.where(lane < STAMP, moved, 0.0)

    @pl.loop(0, stars // UNROLL)
    def _(step):
        placed = []
        for u in range(UNROLL):
            s = step * UNROLL + u
            x = rows_t[pl.ds(s, STAMP, stride=stars), :]
            placed.append((s, pltpu.roll(x, shifts[index, s], axis=1)))
        for s, y in placed:
            spot = pl.ds(spots[index, s], STAMP, stride=stars)
            if lo is None:
                hi[spot, :] = y
            else:
                in_lo = lane32 >= cols[index, s]
                lo[spot, :] = jnp.where(in_lo, y, 0.0)
                hi[spot, :] = jnp.where(in_lo, 0.0, y)


def own_kernel(
    spots, shifts, cols, stamp, root, resid,
    gram, rhs, q_hi, q_lo,
    rows_t, own_lo, own_hi, acc, *, stars, tile_rows,
):
    clear((own_lo, own_hi))
    render(spots, shifts, cols, 0, stamp, rows_t, own_lo, own_hi, stars)
    acc[...] = jnp.zeros_like(acc)

    def group(first, rhs_sum, bottom):
        some = pl.ds(pl.multiple_of(first, GROUP), GROUP)
        root_some, resid_some = root[0, some, :], resid[0, some, :]
        lows, highs = [], []
        for u in range(GROUP):
            y = first + u
            at = pl.ds(pl.multiple_of(y * stars, stars), stars)
            p_lo = own_lo[at, :]
            p_hi = own_hi[at, :]
            rhs_sum = rhs_sum + p_lo * resid_some[u:u + 1, :LANES] + p_hi * resid_some[u:u + 1, LANES:]
            lows.append((p_lo * root_some[u:u + 1, :LANES]).astype(jnp.bfloat16))
            highs.append((p_hi * root_some[u:u + 1, LANES:]).astype(jnp.bfloat16))
            q_hi[0, at, :] = highs[-1]
            if bottom:
                q_lo[0, pl.ds(pl.multiple_of((y - tile_rows) * stars, stars), stars), :] = lows[-1]
        q = jnp.concatenate(lows + highs, axis=1)
        acc[...] += nt_dot(q, q)
        return rhs_sum

    rhs_sum = jnp.zeros((stars, LANES), jnp.float32)
    rhs_sum = lax.fori_loop(0, tile_rows // GROUP, lambda g, r: group(g * GROUP, r, False), rhs_sum)
    rhs_sum = lax.fori_loop(
        0, STAMP // GROUP, lambda g, r: group(tile_rows + g * GROUP, r, True), rhs_sum
    )
    rhs[0] = jnp.sum(rhs_sum, axis=1, keepdims=True)
    gram[0] = acc[...]


def near_kernel(
    spots, shifts, cols, right_st, below_st, diag_st, root, q_hi, q_lo,
    gram,
    rows_t, right_hi, below_lo, below_hi, diag_hi, acc_top, acc_lo, acc_hi,
    *, stars, tile_rows, tile_cols,
):
    edge_lane = tile_cols - LANES
    clear((right_hi, below_lo, below_hi, diag_hi))
    render(spots, shifts, cols, 1, right_st, rows_t, None, right_hi, stars)
    render(spots, shifts, cols, 2, below_st, rows_t, below_lo, below_hi, stars)
    render(spots, shifts, cols, 3, diag_st, rows_t, None, diag_hi, stars)
    acc_top[...] = jnp.zeros_like(acc_top)
    acc_lo[...] = jnp.zeros_like(acc_lo)
    acc_hi[...] = jnp.zeros_like(acc_hi)
    row_lane = lax.broadcasted_iota(jnp.int32, (1, LANES), 1)

    def group(first, bottom):
        some = pl.ds(pl.multiple_of(first, GROUP), GROUP)
        root_some = root[0, some, :]
        parts = {name: [] for name in ("ol", "oh", "rh", "bl", "bh", "dh")}

        def span(y):
            return pl.ds(pl.multiple_of(y * stars, stars), stars)

        for u in range(GROUP):
            at = span(first + u)
            root_lo = root_some[u:u + 1, :LANES]
            root_hi = root_some[u:u + 1, LANES:]
            root_edge = jnp.where(row_lane >= edge_lane, root_hi, 0.0)
            parts["oh"].append(q_hi[0, at, :])
            parts["rh"].append((right_hi[at, :] * root_edge).astype(jnp.bfloat16))
            if bottom:
                at = span(first + u - tile_rows)
                parts["ol"].append(q_lo[0, at, :])
                parts["bl"].append((below_lo[at, :] * root_lo).astype(jnp.bfloat16))
                parts["bh"].append((below_hi[at, :] * root_hi).astype(jnp.bfloat16))
                parts["dh"].append((diag_hi[at, :] * root_edge).astype(jnp.bfloat16))
        q = {name: jnp.concatenate(tiles, axis=1) for name, tiles in parts.items() if tiles}
        if bottom:
            acc_lo[...] += nt_dot(q["ol"], q["bl"])
            acc_hi[...] += nt_dot(
                jnp.concatenate([q["oh"], q["rh"]], axis=0),
                jnp.concatenate([q["rh"], q["bh"], q["dh"]], axis=0),
            )
        else:
            acc_top[...] += nt_dot(q["oh"], q["rh"])

    @pl.loop(0, tile_rows // GROUP)
    def _(g):
        group(g * GROUP, False)

    @pl.loop(0, STAMP // GROUP)
    def _(g):
        group(tile_rows + g * GROUP, True)

    n = stars
    high = acc_hi[...]
    gram[0, 0] = acc_top[...] + high[:n, :n]
    gram[0, 1] = acc_lo[...] + high[:n, n:2 * n]
    gram[0, 2] = high[:n, 2 * n:]
    gram[0, 3] = high[n:, n:2 * n]


def banded(shape):
    return pl.BlockSpec((1,) + shape, lambda b, *_: (b,) + (0,) * len(shape))


def places_of(rows, cols, stars):
    return rows * stars + jnp.arange(stars, dtype=jnp.int32), cols % LANES, cols


def compute_own(places, stamp, root, resid, tile_rows):
    bands, stars, pixels = stamp.shape
    rows_out, cols_out = root.shape[1:]
    tall = pltpu.VMEM((rows_out * stars, LANES), jnp.float32)
    square = (stars, stars)
    strips = ((rows_out * stars, LANES), (STAMP * stars, LANES))

    def kernel(*refs):
        own_kernel(*refs, stars=stars, tile_rows=tile_rows)

    return pl.pallas_call(
        kernel,
        out_shape=(
            jax.ShapeDtypeStruct((bands,) + square, jnp.float32),
            jax.ShapeDtypeStruct((bands, stars, 1), jnp.float32),
            jax.ShapeDtypeStruct((bands,) + strips[0], jnp.bfloat16),
            jax.ShapeDtypeStruct((bands,) + strips[1], jnp.bfloat16),
        ),
        grid_spec=pltpu.PrefetchScalarGridSpec(
            num_scalar_prefetch=3,
            grid=(bands,),
            in_specs=[banded((stars, pixels))] + [banded((rows_out, cols_out))] * 2,
            out_specs=(banded(square), banded((stars, 1)), banded(strips[0]), banded(strips[1])),
            scratch_shapes=[
                pltpu.VMEM((STAMP * stars, LANES), jnp.float32), tall, tall,
                pltpu.VMEM(square, jnp.float32),
            ],
        ),
        compiler_params=pltpu.CompilerParams(vmem_limit_bytes=24 << 20),
        cost_estimate=pl.CostEstimate(flops=20 * 10**9, bytes_accessed=60 * 10**6, transcendentals=0),
        name="own",
    )(*places, stamp, root, resid)


def compute_near(places, stamp_sets, root, q_hi, q_lo, tile_rows, tile_cols):
    bands, stars, pixels = stamp_sets[0].shape
    rows_out, cols_out = root.shape[1:]
    tall = pltpu.VMEM((rows_out * stars, LANES), jnp.float32)
    short = pltpu.VMEM((2 * STAMP * stars, LANES), jnp.float32)

    def kernel(*refs):
        near_kernel(*refs, stars=stars, tile_rows=tile_rows, tile_cols=tile_cols)

    return pl.pallas_call(
        kernel,
        out_shape=jax.ShapeDtypeStruct((bands, 4, stars, stars), jnp.float32),
        grid_spec=pltpu.PrefetchScalarGridSpec(
            num_scalar_prefetch=3,
            grid=(bands,),
            in_specs=[banded((stars, pixels))] * 3
            + [banded((rows_out, cols_out)), banded(q_hi.shape[1:]), banded(q_lo.shape[1:])],
            out_specs=banded((4, stars, stars)),
            scratch_shapes=[
                pltpu.VMEM((STAMP * stars, LANES), jnp.float32), tall, short, short, short,
                pltpu.VMEM((stars, stars), jnp.float32),
                pltpu.VMEM((stars, stars), jnp.float32),
                pltpu.VMEM((2 * stars, 3 * stars), jnp.float32),
            ],
        ),
        compiler_params=pltpu.CompilerParams(vmem_limit_bytes=28 << 20),
        cost_estimate=pl.CostEstimate(flops=20 * 10**9, bytes_accessed=60 * 10**6, transcendentals=0),
        name="near",
    )(*places, *stamp_sets, root, q_hi, q_lo)


def body(stamps, positions, weights, mask, residual):
    band_count, tile_rows, tile_cols = weights.shape
    star_count = stamps.shape[3]
    half_side = STAMP // 2
    rows_out = tile_rows + STAMP
    cols_out = tile_cols + STAMP
    own, places = stamps[0, 0], positions[0, 0]
    right_st = shifted(own, "tx", -1)
    near_places = shifted(places, "tx", -1)
    low_places = shifted(jnp.stack([places, near_places]), "ty", -1)
    right = (right_st, near_places)
    below = (shifted(own, "ty", -1), low_places[0])
    diag = (shifted(right_st, "ty", -1), low_places[1])

    weight = weights * mask.astype(jnp.float32)
    fields = jnp.stack((jnp.sqrt(weight), weight * residual)).astype(jnp.bfloat16)
    region = padded(fields, (("ty", 2), ("tx", 3)), half_side).astype(jnp.float32)

    anchor_row = lax.axis_index("ty") * tile_rows
    anchor_col = lax.axis_index("tx") * tile_cols

    def rows_of(pair):
        return pair[1][0] - anchor_row

    def cols_of(pair):
        return pair[1][1] - anchor_col

    mine = (own, places)
    own_places = places_of(
        jnp.clip(rows_of(mine), 0, tile_rows)[None], jnp.clip(cols_of(mine), 0, tile_cols)[None], star_count
    )
    zero = jnp.zeros((star_count,), jnp.int32)
    rows = jnp.stack([
        zero,
        jnp.clip(rows_of(right), 0, tile_rows),
        jnp.clip(rows_of(below) - tile_rows, 0, STAMP),
        jnp.clip(rows_of(diag) - tile_rows, 0, STAMP),
    ])
    cols = jnp.stack([
        zero,
        jnp.clip(cols_of(right), tile_cols, cols_out),
        jnp.clip(cols_of(below), 0, tile_cols),
        jnp.clip(cols_of(diag), tile_cols, cols_out),
    ])
    root, resid = region[0], region[1]
    self_own, rhs, q_hi, q_lo = compute_own(own_places, own, root, resid, tile_rows)
    blocks = compute_near(
        places_of(rows, cols, star_count), (right[0], below[0], diag[0]), root, q_hi, q_lo,
        tile_rows, tile_cols,
    )
    own_right, own_below, own_diag, right_below = [blocks[:, i] for i in range(4)]
    to_right = jnp.stack(
        [jnp.swapaxes(own_right, 1, 2), right_below, jnp.swapaxes(own_diag, 1, 2)]
    ).astype(jnp.bfloat16)
    from_left = shifted(to_right, "tx", 1)
    to_below = jnp.stack([jnp.swapaxes(own_below, 1, 2), jnp.swapaxes(right_below, 1, 2)])
    from_above, corner = shifted((to_below, from_left[2]), "ty", 1)
    from_left = from_left.astype(jnp.float32)
    gram = jnp.concatenate(
        [
            corner.astype(jnp.float32), from_above[0], from_above[1],
            from_left[0], self_own, own_right,
            from_left[1], own_below, own_diag,
        ],
        axis=2,
    )
    return (
        gram.reshape(1, 1, band_count, star_count, 9 * star_count),
        rhs.reshape(1, 1, band_count, star_count),
    )


def solution(mesh):
    return jax.shard_map(
        body,
        mesh=mesh,
        in_specs=(
            P("ty", "tx", None, None, None),
            P("ty", "tx", None, None),
            P(None, "ty", "tx"),
            P(None, "ty", "tx"),
            P(None, "ty", "tx"),
        ),
        out_specs=(P("ty", "tx", None, None, None), P("ty", "tx", None, None)),
        check_vma=False,
    )
```

```python
import jax
import jax.numpy as jnp
from jax import lax
from jax.experimental import pallas as pl
from jax.experimental.pallas import tpu as pltpu
from jax.sharding import PartitionSpec as P

STAMP = 32
LANES = 128
GROUP = 8
UNROLL = 16


def padded(cells, sides, width):
    for axis, dim in sides:
        count = lax.axis_size(axis)
        ends = count - 1
        head = lax.slice_in_dim(cells, 0, width, axis=dim)
        tail = lax.slice_in_dim(cells, cells.shape[dim] - width, cells.shape[dim], axis=dim)
        cells = jnp.concatenate(
            [
                lax.ppermute(tail, axis, [(i, i + 1) for i in range(ends)]),
                cells,
                lax.ppermute(head, axis, [(i + 1, i) for i in range(ends)]),
            ],
            axis=dim,
        )
    return cells


def shifted(x, axis, by):
    length = lax.axis_size(axis)
    pairs = [(i, i + by) for i in range(length) if 0 <= i + by < length]
    return lax.ppermute(x, axis, pairs)


def moved(x, down, along):
    rows, cols = lax.axis_size("ty"), lax.axis_size("tx")
    pairs = [
        (a * cols + c, (a + down) * cols + c + along)
        for a in range(rows) for c in range(cols)
        if 0 <= a + down < rows and 0 <= c + along < cols
    ]
    return lax.ppermute(x, ("ty", "tx"), pairs)


def nt_dot(left, right):
    return lax.dot_general(left, right, (((1,), (1,)), ((), ())), preferred_element_type=jnp.float32)


def clear(refs):
    @pl.when(pl.program_id(0) == 0)
    def _():
        for ref in refs:
            @pl.loop(0, ref.shape[0] // 512)
            def _(i):
                ref[pl.ds(pl.multiple_of(i * 512, 512), 512), :] = jnp.zeros((512, LANES), jnp.float32)


def render(spots, shifts, cols, index, stamp_ref, rows_t, lo, hi, stars):
    lane = lax.broadcasted_iota(jnp.int32, (stars, LANES), 1)
    lane32 = lax.broadcasted_iota(jnp.int32, (STAMP, LANES), 1)
    per_tile = LANES // STAMP
    for k in range(STAMP // per_tile):
        x = stamp_ref[0, :, k * LANES:(k + 1) * LANES].astype(jnp.float32)
        for j in range(per_tile):
            moved = x if j == 0 else pltpu.roll(x, LANES - STAMP * j, axis=1)
            row = k * per_tile + j
            rows_t[row * stars:(row + 1) * stars, :] = jnp.where(lane < STAMP, moved, 0.0)

    @pl.loop(0, stars // UNROLL)
    def _(step):
        placed = []
        for u in range(UNROLL):
            s = step * UNROLL + u
            x = rows_t[pl.ds(s, STAMP, stride=stars), :]
            placed.append((s, pltpu.roll(x, shifts[index, s], axis=1)))
        for s, y in placed:
            spot = pl.ds(spots[index, s], STAMP, stride=stars)
            if lo is None:
                hi[spot, :] = y
            else:
                in_lo = lane32 >= cols[index, s]
                lo[spot, :] = jnp.where(in_lo, y, 0.0)
                hi[spot, :] = jnp.where(in_lo, 0.0, y)


def own_kernel(
    spots, shifts, cols, stamp, root, resid,
    gram, rhs, q_hi, q_lo,
    rows_t, own_lo, own_hi, acc, *, stars, tile_rows,
):
    clear((own_lo, own_hi))
    render(spots, shifts, cols, 0, stamp, rows_t, own_lo, own_hi, stars)
    acc[...] = jnp.zeros_like(acc)

    def group(first, rhs_sum, bottom):
        some = pl.ds(pl.multiple_of(first, GROUP), GROUP)
        root_some, resid_some = root[0, some, :], resid[0, some, :]
        lows, highs = [], []
        for u in range(GROUP):
            y = first + u
            at = pl.ds(pl.multiple_of(y * stars, stars), stars)
            p_lo = own_lo[at, :]
            p_hi = own_hi[at, :]
            rhs_sum = rhs_sum + p_lo * resid_some[u:u + 1, :LANES] + p_hi * resid_some[u:u + 1, LANES:]
            lows.append((p_lo * root_some[u:u + 1, :LANES]).astype(jnp.bfloat16))
            highs.append((p_hi * root_some[u:u + 1, LANES:]).astype(jnp.bfloat16))
            q_hi[0, at, :] = highs[-1]
            if bottom:
                q_lo[0, pl.ds(pl.multiple_of((y - tile_rows) * stars, stars), stars), :] = lows[-1]
        q = jnp.concatenate(lows + highs, axis=1)
        acc[...] += nt_dot(q, q)
        return rhs_sum

    rhs_sum = jnp.zeros((stars, LANES), jnp.float32)
    rhs_sum = lax.fori_loop(0, tile_rows // GROUP, lambda g, r: group(g * GROUP, r, False), rhs_sum)
    rhs_sum = lax.fori_loop(
        0, STAMP // GROUP, lambda g, r: group(tile_rows + g * GROUP, r, True), rhs_sum
    )
    rhs[0] = jnp.sum(rhs_sum, axis=1, keepdims=True)
    gram[0] = acc[...]


def near_kernel(
    spots, shifts, cols, right_st, below_st, diag_st, root, q_hi, q_lo,
    gram,
    rows_t, right_hi, below_lo, below_hi, diag_hi, acc_top, acc_lo, acc_hi,
    *, stars, tile_rows, tile_cols,
):
    edge_lane = tile_cols - LANES
    clear((right_hi, below_lo, below_hi, diag_hi))
    render(spots, shifts, cols, 1, right_st, rows_t, None, right_hi, stars)
    render(spots, shifts, cols, 2, below_st, rows_t, below_lo, below_hi, stars)
    render(spots, shifts, cols, 3, diag_st, rows_t, None, diag_hi, stars)
    acc_top[...] = jnp.zeros_like(acc_top)
    acc_lo[...] = jnp.zeros_like(acc_lo)
    acc_hi[...] = jnp.zeros_like(acc_hi)
    row_lane = lax.broadcasted_iota(jnp.int32, (1, LANES), 1)

    def group(first, bottom):
        some = pl.ds(pl.multiple_of(first, GROUP), GROUP)
        root_some = root[0, some, :]
        parts = {name: [] for name in ("ol", "oh", "rh", "bl", "bh", "dh")}

        def span(y):
            return pl.ds(pl.multiple_of(y * stars, stars), stars)

        for u in range(GROUP):
            at = span(first + u)
            root_lo = root_some[u:u + 1, :LANES]
            root_hi = root_some[u:u + 1, LANES:]
            root_edge = jnp.where(row_lane >= edge_lane, root_hi, 0.0)
            parts["oh"].append(q_hi[0, at, :])
            parts["rh"].append((right_hi[at, :] * root_edge).astype(jnp.bfloat16))
            if bottom:
                at = span(first + u - tile_rows)
                parts["ol"].append(q_lo[0, at, :])
                parts["bl"].append((below_lo[at, :] * root_lo).astype(jnp.bfloat16))
                parts["bh"].append((below_hi[at, :] * root_hi).astype(jnp.bfloat16))
                parts["dh"].append((diag_hi[at, :] * root_edge).astype(jnp.bfloat16))
        q = {name: jnp.concatenate(tiles, axis=1) for name, tiles in parts.items() if tiles}
        if bottom:
            acc_lo[...] += nt_dot(q["ol"], q["bl"])
            acc_hi[...] += nt_dot(
                jnp.concatenate([q["oh"], q["rh"]], axis=0),
                jnp.concatenate([q["rh"], q["bh"], q["dh"]], axis=0),
            )
        else:
            acc_top[...] += nt_dot(q["oh"], q["rh"])

    @pl.loop(0, tile_rows // GROUP)
    def _(g):
        group(g * GROUP, False)

    @pl.loop(0, STAMP // GROUP)
    def _(g):
        group(tile_rows + g * GROUP, True)

    n = stars
    high = acc_hi[...]
    gram[0, 0] = acc_top[...] + high[:n, :n]
    gram[0, 1] = acc_lo[...] + high[:n, n:2 * n]
    gram[0, 2] = high[:n, 2 * n:]
    gram[0, 3] = high[n:, n:2 * n]


def banded(shape):
    return pl.BlockSpec((1,) + shape, lambda b, *_: (b,) + (0,) * len(shape))


def places_of(rows, cols, stars):
    return rows * stars + jnp.arange(stars, dtype=jnp.int32), cols % LANES, cols


def compute_own(places, stamp, root, resid, tile_rows):
    bands, stars, pixels = stamp.shape
    rows_out, cols_out = root.shape[1:]
    tall = pltpu.VMEM((rows_out * stars, LANES), jnp.float32)
    square = (stars, stars)
    strips = ((rows_out * stars, LANES), (STAMP * stars, LANES))

    def kernel(*refs):
        own_kernel(*refs, stars=stars, tile_rows=tile_rows)

    return pl.pallas_call(
        kernel,
        out_shape=(
            jax.ShapeDtypeStruct((bands,) + square, jnp.float32),
            jax.ShapeDtypeStruct((bands, stars, 1), jnp.float32),
            jax.ShapeDtypeStruct((bands,) + strips[0], jnp.bfloat16),
            jax.ShapeDtypeStruct((bands,) + strips[1], jnp.bfloat16),
        ),
        grid_spec=pltpu.PrefetchScalarGridSpec(
            num_scalar_prefetch=3,
            grid=(bands,),
            in_specs=[banded((stars, pixels))] + [banded((rows_out, cols_out))] * 2,
            out_specs=(banded(square), banded((stars, 1)), banded(strips[0]), banded(strips[1])),
            scratch_shapes=[
                pltpu.VMEM((STAMP * stars, LANES), jnp.float32), tall, tall,
                pltpu.VMEM(square, jnp.float32),
            ],
        ),
        compiler_params=pltpu.CompilerParams(vmem_limit_bytes=56 << 20),
        cost_estimate=pl.CostEstimate(flops=20 * 10**9, bytes_accessed=60 * 10**6, transcendentals=0),
        name="own",
    )(*places, stamp, root, resid)


def compute_near(places, stamp_sets, root, q_hi, q_lo, tile_rows, tile_cols):
    bands, stars, pixels = stamp_sets[0].shape
    rows_out, cols_out = root.shape[1:]
    tall = pltpu.VMEM((rows_out * stars, LANES), jnp.float32)
    short = pltpu.VMEM((2 * STAMP * stars, LANES), jnp.float32)

    def kernel(*refs):
        near_kernel(*refs, stars=stars, tile_rows=tile_rows, tile_cols=tile_cols)

    return pl.pallas_call(
        kernel,
        out_shape=jax.ShapeDtypeStruct((bands, 4, stars, stars), jnp.float32),
        grid_spec=pltpu.PrefetchScalarGridSpec(
            num_scalar_prefetch=3,
            grid=(bands,),
            in_specs=[banded((stars, pixels))] * 3
            + [banded((rows_out, cols_out)), banded(q_hi.shape[1:]), banded(q_lo.shape[1:])],
            out_specs=banded((4, stars, stars)),
            scratch_shapes=[
                pltpu.VMEM((STAMP * stars, LANES), jnp.float32), tall, short, short, short,
                pltpu.VMEM((stars, stars), jnp.float32),
                pltpu.VMEM((stars, stars), jnp.float32),
                pltpu.VMEM((2 * stars, 3 * stars), jnp.float32),
            ],
        ),
        compiler_params=pltpu.CompilerParams(vmem_limit_bytes=56 << 20),
        cost_estimate=pl.CostEstimate(flops=20 * 10**9, bytes_accessed=60 * 10**6, transcendentals=0),
        name="near",
    )(*places, *stamp_sets, root, q_hi, q_lo)


def body(stamps, positions, weights, mask, residual):
    band_count, tile_rows, tile_cols = weights.shape
    star_count = stamps.shape[3]
    half_side = STAMP // 2
    rows_out = tile_rows + STAMP
    cols_out = tile_cols + STAMP
    own, places = stamps[0, 0], positions[0, 0]
    near_places = shifted(places, "tx", -1)
    low_places = shifted(places, "ty", -1)
    diag_places = moved(places, -1, -1)
    weight = weights * mask.astype(jnp.float32)
    fields = jnp.stack((jnp.sqrt(weight), weight * residual)).astype(jnp.bfloat16)
    region = padded(fields, (("ty", 2), ("tx", 3)), half_side).astype(jnp.float32)

    region, sent = lax.optimization_barrier((region, own))
    right = (shifted(sent, "tx", -1), near_places)
    below = (shifted(sent, "ty", -1), low_places)
    diag = (moved(sent, -1, -1), diag_places)

    anchor_row = lax.axis_index("ty") * tile_rows
    anchor_col = lax.axis_index("tx") * tile_cols

    def rows_of(pair):
        return pair[1][0] - anchor_row

    def cols_of(pair):
        return pair[1][1] - anchor_col

    mine = (own, places)
    own_places = places_of(
        jnp.clip(rows_of(mine), 0, tile_rows)[None], jnp.clip(cols_of(mine), 0, tile_cols)[None], star_count
    )
    zero = jnp.zeros((star_count,), jnp.int32)
    rows = jnp.stack([
        zero,
        jnp.clip(rows_of(right), 0, tile_rows),
        jnp.clip(rows_of(below) - tile_rows, 0, STAMP),
        jnp.clip(rows_of(diag) - tile_rows, 0, STAMP),
    ])
    cols = jnp.stack([
        zero,
        jnp.clip(cols_of(right), tile_cols, cols_out),
        jnp.clip(cols_of(below), 0, tile_cols),
        jnp.clip(cols_of(diag), tile_cols, cols_out),
    ])
    root, resid = region[0], region[1]
    self_own, rhs, q_hi, q_lo = compute_own(own_places, own, root, resid, tile_rows)
    blocks = compute_near(
        places_of(rows, cols, star_count), (right[0], below[0], diag[0]), root, q_hi, q_lo,
        tile_rows, tile_cols,
    )
    own_right, own_below, own_diag, right_below = [blocks[:, i] for i in range(4)]
    to_right = jnp.stack([jnp.swapaxes(own_right, 1, 2), right_below]).astype(jnp.bfloat16)
    to_below = jnp.stack([jnp.swapaxes(own_below, 1, 2), jnp.swapaxes(right_below, 1, 2)])
    from_left = shifted(to_right, "tx", 1).astype(jnp.float32)
    from_above = shifted(to_below, "ty", 1)
    corner = moved(jnp.swapaxes(own_diag, 1, 2).astype(jnp.bfloat16), 1, 1)
    gram = jnp.concatenate(
        [
            corner.astype(jnp.float32), from_above[0], from_above[1],
            from_left[0], self_own, own_right,
            from_left[1], own_below, own_diag,
        ],
        axis=2,
    )
    return (
        gram.reshape(1, 1, band_count, star_count, 9 * star_count),
        rhs.reshape(1, 1, band_count, star_count),
    )


def solution(mesh):
    return jax.shard_map(
        body,
        mesh=mesh,
        in_specs=(
            P("ty", "tx", None, None, None),
            P("ty", "tx", None, None),
            P(None, "ty", "tx"),
            P(None, "ty", "tx"),
            P(None, "ty", "tx"),
        ),
        out_specs=(P("ty", "tx", None, None, None), P("ty", "tx", None, None)),
        check_vma=False,
    )
```

```python
import jax
import jax.numpy as jnp
from jax import lax
from jax.experimental import pallas as pl
from jax.experimental.pallas import tpu as pltpu
from jax.sharding import PartitionSpec as P

STAMP = 32
LANES = 128
GROUP = 8
UNROLL = 8


def padded(cells, sides, width):
    for axis, dim in sides:
        count = lax.axis_size(axis)
        ends = count - 1
        head = lax.slice_in_dim(cells, 0, width, axis=dim)
        tail = lax.slice_in_dim(cells, cells.shape[dim] - width, cells.shape[dim], axis=dim)
        cells = jnp.concatenate(
            [
                lax.ppermute(tail, axis, [(i, i + 1) for i in range(ends)]),
                cells,
                lax.ppermute(head, axis, [(i + 1, i) for i in range(ends)]),
            ],
            axis=dim,
        )
    return cells


def shifted(x, axis, by):
    length = lax.axis_size(axis)
    pairs = [(i, i + by) for i in range(length) if 0 <= i + by < length]
    return lax.ppermute(x, axis, pairs)


def moved(x, down, along):
    rows, cols = lax.axis_size("ty"), lax.axis_size("tx")
    pairs = [
        (a * cols + c, (a + down) * cols + c + along)
        for a in range(rows) for c in range(cols)
        if 0 <= a + down < rows and 0 <= c + along < cols
    ]
    return lax.ppermute(x, ("ty", "tx"), pairs)


def nt_dot(left, right):
    return lax.dot_general(left, right, (((1,), (1,)), ((), ())), preferred_element_type=jnp.float32)


def gram_kernel(
    starts, own_st, right_st, below_st, diag_st, root, resid,
    gram, rhs,
    rows_t, own_lo, own_hi, right_hi, below_lo, below_hi, diag_hi, acc_top, acc_lo, acc_hi,
    listed, counts, *, stars, tile_rows, tile_cols,
):
    edge_lane = tile_cols - LANES

    @pl.when(pl.program_id(0) == 0)
    def _():
        for ref in (own_lo, own_hi, right_hi, below_lo, below_hi, diag_hi):
            @pl.loop(0, ref.shape[0] // 512)
            def _(i):
                ref[pl.ds(pl.multiple_of(i * 512, 512), 512), :] = jnp.zeros((512, LANES), jnp.float32)

        for index in range(1, 4):
            @pl.loop(0, stars + UNROLL)
            def _(s):
                listed[index, s] = 0

            def listing(s, count):
                reaches = starts[index, 1, s] < tile_cols + STAMP
                if index > 1:
                    reaches = reaches & (starts[index, 0, s] < STAMP)
                listed[index, count] = s
                return count + reaches.astype(jnp.int32)

            counts[index] = lax.fori_loop(0, stars, listing, 0)

    lane = lax.broadcasted_iota(jnp.int32, (stars, LANES), 1)
    lane32 = lax.broadcasted_iota(jnp.int32, (STAMP, LANES), 1)
    per_tile = LANES // STAMP

    for index, (stamp_ref, lo, hi) in enumerate(
        ((own_st, own_lo, own_hi), (right_st, None, right_hi), (below_st, below_lo, below_hi), (diag_st, None, diag_hi))
    ):
        for k in range(STAMP // per_tile):
            x = stamp_ref[0, :, k * LANES:(k + 1) * LANES].astype(jnp.float32)
            for j in range(per_tile):
                moved = x if j == 0 else pltpu.roll(x, LANES - STAMP * j, axis=1)
                row = k * per_tile + j
                rows_t[row * stars:(row + 1) * stars, :] = jnp.where(lane < STAMP, moved, 0.0)

        batches = stars // UNROLL if index == 0 else (counts[index] + UNROLL - 1) // UNROLL

        @pl.loop(0, batches)
        def _(step):
            placed = []
            for u in range(UNROLL):
                s = step * UNROLL + u
                if index:
                    s = listed[index, s]
                x = rows_t[pl.ds(s, STAMP, stride=stars), :]
                col = starts[index, 1, s]
                y = pltpu.roll(x, lax.rem(col, LANES), axis=1)
                placed.append((pl.ds(starts[index, 0, s] * stars + s, STAMP, stride=stars), col, y))
            for spot, col, y in placed:
                if lo is None:
                    hi[spot, :] = y
                else:
                    in_lo = lane32 >= col
                    lo[spot, :] = jnp.where(in_lo, y, 0.0)
                    hi[spot, :] = jnp.where(in_lo, 0.0, y)

    acc_top[...] = jnp.zeros_like(acc_top)
    acc_lo[...] = jnp.zeros_like(acc_lo)
    acc_hi[...] = jnp.zeros_like(acc_hi)
    row_lane = lax.broadcasted_iota(jnp.int32, (1, LANES), 1)

    def weigh(ref, y, factor):
        return (ref[pl.ds(pl.multiple_of(y * stars, stars), stars), :] * factor).astype(jnp.bfloat16)

    def group(first, rhs_sum, bottom):
        parts = {name: [] for name in ("ol", "oh", "rh", "bl", "bh", "dh")}
        some = pl.ds(pl.multiple_of(first, GROUP), GROUP)
        root_some, resid_some = root[0, some, :], resid[0, some, :]
        for u in range(GROUP):
            y = first + u
            root_lo = root_some[u:u + 1, :LANES]
            root_hi = root_some[u:u + 1, LANES:]
            root_edge = jnp.where(row_lane >= edge_lane, root_hi, 0.0)
            at = pl.ds(pl.multiple_of(y * stars, stars), stars)
            p_lo = own_lo[at, :]
            p_hi = own_hi[at, :]
            rhs_sum = rhs_sum + p_lo * resid_some[u:u + 1, :LANES] + p_hi * resid_some[u:u + 1, LANES:]
            parts["ol"].append((p_lo * root_lo).astype(jnp.bfloat16))
            parts["oh"].append((p_hi * root_hi).astype(jnp.bfloat16))
            parts["rh"].append(weigh(right_hi, y, root_edge))
            if bottom:
                parts["bl"].append(weigh(below_lo, y - tile_rows, root_lo))
                parts["bh"].append(weigh(below_hi, y - tile_rows, root_hi))
                parts["dh"].append(weigh(diag_hi, y - tile_rows, root_edge))
        q = {name: jnp.concatenate(tiles, axis=1) for name, tiles in parts.items() if tiles}
        if bottom:
            acc_lo[...] += nt_dot(q["ol"], jnp.concatenate([q["ol"], q["bl"]], axis=0))
            four = jnp.concatenate([q["oh"], q["rh"], q["bh"], q["dh"]], axis=0)
            acc_hi[...] += nt_dot(four[:2 * stars], four)
        else:
            acc_top[...] += nt_dot(q["oh"], jnp.concatenate([q["oh"], q["rh"]], axis=0))
            acc_lo[:, :stars] += nt_dot(q["ol"], q["ol"])
        return rhs_sum

    rhs_sum = jnp.zeros((stars, LANES), jnp.float32)
    rhs_sum = lax.fori_loop(0, tile_rows // GROUP, lambda g, r: group(g * GROUP, r, False), rhs_sum)
    rhs_sum = lax.fori_loop(
        0, STAMP // GROUP, lambda g, r: group(tile_rows + g * GROUP, r, True), rhs_sum
    )
    rhs[0] = jnp.sum(rhs_sum, axis=1, keepdims=True)
    n = stars
    top, low, high = acc_top[...], acc_lo[...], acc_hi[...]
    gram[0, 0] = low[:, :n] + top[:, :n] + high[:n, :n]
    gram[0, 1] = top[:, n:2 * n] + high[:n, n:2 * n]
    gram[0, 2] = low[:, n:2 * n] + high[:n, 2 * n:3 * n]
    gram[0, 3] = high[:n, 3 * n:]
    gram[0, 4] = high[n:, 2 * n:3 * n]


def compute(starts, stamp_sets, root, resid, tile_rows, tile_cols):
    bands, stars, pixels = stamp_sets[0].shape
    rows_out, cols_out = root.shape[1:]
    stamp_spec = pl.BlockSpec((1, stars, pixels), lambda b, st: (b, 0, 0))
    field_spec = pl.BlockSpec((1, rows_out, cols_out), lambda b, st: (b, 0, 0))
    tall = pltpu.VMEM((rows_out * stars, LANES), jnp.float32)
    short = pltpu.VMEM((2 * STAMP * stars, LANES), jnp.float32)

    def kernel(*refs):
        gram_kernel(*refs, stars=stars, tile_rows=tile_rows, tile_cols=tile_cols)

    return pl.pallas_call(
        kernel,
        out_shape=(
            jax.ShapeDtypeStruct((bands, 5, stars, stars), jnp.float32),
            jax.ShapeDtypeStruct((bands, stars, 1), jnp.float32),
        ),
        grid_spec=pltpu.PrefetchScalarGridSpec(
            num_scalar_prefetch=1,
            grid=(bands,),
            in_specs=[stamp_spec] * 4 + [field_spec] * 2,
            out_specs=(
                pl.BlockSpec((1, 5, stars, stars), lambda b, st: (b, 0, 0, 0)),
                pl.BlockSpec((1, stars, 1), lambda b, st: (b, 0, 0)),
            ),
            scratch_shapes=[
                pltpu.VMEM((STAMP * stars, LANES), jnp.float32),
                tall, tall, tall, short, short, short,
                pltpu.VMEM((stars, 2 * stars), jnp.float32),
                pltpu.VMEM((stars, 2 * stars), jnp.float32),
                pltpu.VMEM((2 * stars, 4 * stars), jnp.float32),
                pltpu.SMEM((4, stars + UNROLL), jnp.int32),
                pltpu.SMEM((4,), jnp.int32),
            ],
        ),
        compiler_params=pltpu.CompilerParams(vmem_limit_bytes=40 << 20),
        name="gram",
    )(starts, *stamp_sets, root, resid)


def body(stamps, positions, weights, mask, residual):
    band_count, tile_rows, tile_cols = weights.shape
    star_count = stamps.shape[3]
    half_side = STAMP // 2
    rows_out = tile_rows + STAMP
    cols_out = tile_cols + STAMP
    own, places = stamps[0, 0], positions[0, 0]
    right = shifted((own, places), "tx", -1)
    below = shifted((own, places), "ty", -1)
    diag = (moved(own, -1, -1), moved(places, -1, -1))

    weight = weights * mask.astype(jnp.float32)
    fields = jnp.stack((jnp.sqrt(weight), weight * residual)).astype(jnp.bfloat16)
    region = padded(fields, (("ty", 2), ("tx", 3)), half_side).astype(jnp.float32)

    anchor_row = lax.axis_index("ty") * tile_rows
    anchor_col = lax.axis_index("tx") * tile_cols

    def rows_of(pair):
        return pair[1][0] - anchor_row

    def cols_of(pair):
        return pair[1][1] - anchor_col

    mine = (own, places)
    has_right = lax.axis_index("tx") < lax.axis_size("tx") - 1
    has_below = lax.axis_index("ty") < lax.axis_size("ty") - 1

    def strip_cols(pair):
        return jnp.where(has_right, jnp.clip(cols_of(pair), tile_cols, cols_out), cols_out)

    def strip_rows(pair):
        return jnp.where(has_below, jnp.clip(rows_of(pair) - tile_rows, 0, STAMP), STAMP)

    starts = jnp.stack([
        jnp.stack([jnp.clip(rows_of(mine), 0, tile_rows), jnp.clip(cols_of(mine), 0, tile_cols)]),
        jnp.stack([jnp.clip(rows_of(right), 0, tile_rows), strip_cols(right)]),
        jnp.stack([strip_rows(below), jnp.clip(cols_of(below), 0, tile_cols)]),
        jnp.stack([strip_rows(diag), strip_cols(diag)]),
    ])
    blocks, rhs = compute(
        starts, (own, right[0], below[0], diag[0]), region[0], region[1], tile_rows, tile_cols
    )
    self_own, own_right, own_below, own_diag, right_below = [blocks[:, i] for i in range(5)]
    to_right = jnp.stack([jnp.swapaxes(own_right, 1, 2), right_below]).astype(jnp.bfloat16)
    to_below = jnp.stack([jnp.swapaxes(own_below, 1, 2), jnp.swapaxes(right_below, 1, 2)])
    from_left = shifted(to_right, "tx", 1).astype(jnp.float32)
    from_above = shifted(to_below, "ty", 1)
    corner = moved(jnp.swapaxes(own_diag, 1, 2).astype(jnp.bfloat16), 1, 1)
    gram = jnp.concatenate(
        [
            corner.astype(jnp.float32), from_above[0], from_above[1],
            from_left[0], self_own, own_right,
            from_left[1], own_below, own_diag,
        ],
        axis=2,
    )
    return (
        gram.reshape(1, 1, band_count, star_count, 9 * star_count),
        rhs.reshape(1, 1, band_count, star_count),
    )


def solution(mesh):
    return jax.shard_map(
        body,
        mesh=mesh,
        in_specs=(
            P("ty", "tx", None, None, None),
            P("ty", "tx", None, None),
            P(None, "ty", "tx"),
            P(None, "ty", "tx"),
            P(None, "ty", "tx"),
        ),
        out_specs=(P("ty", "tx", None, None, None), P("ty", "tx", None, None)),
        check_vma=False,
    )
```

```python
import jax
import jax.numpy as jnp
from jax import lax
from jax.experimental import pallas as pl
from jax.experimental.pallas import tpu as pltpu
from jax.sharding import PartitionSpec as P

STAMP = 32
LANES = 128
GROUP = 8
UNROLL = 8


def padded(cells, sides, width):
    for axis, dim in sides:
        count = lax.axis_size(axis)
        ends = count - 1
        head = lax.slice_in_dim(cells, 0, width, axis=dim)
        tail = lax.slice_in_dim(cells, cells.shape[dim] - width, cells.shape[dim], axis=dim)
        cells = jnp.concatenate(
            [
                lax.ppermute(tail, axis, [(i, i + 1) for i in range(ends)]),
                cells,
                lax.ppermute(head, axis, [(i + 1, i) for i in range(ends)]),
            ],
            axis=dim,
        )
    return cells


def shifted(x, axis, by):
    length = lax.axis_size(axis)
    pairs = [(i, i + by) for i in range(length) if 0 <= i + by < length]
    return lax.ppermute(x, axis, pairs)


def moved(x, down, along):
    rows, cols = lax.axis_size("ty"), lax.axis_size("tx")
    pairs = [
        (a * cols + c, (a + down) * cols + c + along)
        for a in range(rows) for c in range(cols)
        if 0 <= a + down < rows and 0 <= c + along < cols
    ]
    return lax.ppermute(x, ("ty", "tx"), pairs)


def nt_dot(left, right):
    return lax.dot_general(left, right, (((1,), (1,)), ((), ())), preferred_element_type=jnp.float32)


def gram_kernel(
    starts, own_st, right_st, below_st, diag_st, root, resid,
    gram, rhs,
    rows_t, own_lo, own_hi, right_hi, below_lo, below_hi, diag_hi, acc_top, acc_lo, acc_hi,
    listed, counts, *, stars, tile_rows, tile_cols,
):
    edge_lane = tile_cols - LANES

    @pl.when(pl.program_id(0) == 0)
    def _():
        for ref in (own_lo, own_hi, right_hi, below_lo, below_hi, diag_hi):
            @pl.loop(0, ref.shape[0] // 512)
            def _(i):
                ref[pl.ds(pl.multiple_of(i * 512, 512), 512), :] = jnp.zeros((512, LANES), jnp.float32)

        for index in range(1, 4):
            @pl.loop(0, stars + UNROLL)
            def _(s):
                listed[index, s] = 0

            def listing(s, count):
                reaches = starts[index, 1, s] < tile_cols + STAMP
                if index > 1:
                    reaches = reaches & (starts[index, 0, s] < STAMP)
                listed[index, count] = s
                return count + reaches.astype(jnp.int32)

            counts[index] = lax.fori_loop(0, stars, listing, 0)

    lane = lax.broadcasted_iota(jnp.int32, (stars, LANES), 1)
    lane32 = lax.broadcasted_iota(jnp.int32, (STAMP, LANES), 1)
    per_tile = LANES // STAMP

    for index, (stamp_ref, lo, hi) in enumerate(
        ((own_st, own_lo, own_hi), (right_st, None, right_hi), (below_st, below_lo, below_hi), (diag_st, None, diag_hi))
    ):
        for k in range(STAMP // per_tile):
            x = stamp_ref[0, :, k * LANES:(k + 1) * LANES].astype(jnp.float32)
            for j in range(per_tile):
                moved = x if j == 0 else pltpu.roll(x, LANES - STAMP * j, axis=1)
                row = k * per_tile + j
                rows_t[row * stars:(row + 1) * stars, :] = jnp.where(lane < STAMP, moved, 0.0)

        batches = stars // UNROLL if index == 0 else (counts[index] + UNROLL - 1) // UNROLL

        @pl.loop(0, batches)
        def _(step):
            placed = []
            for u in range(UNROLL):
                s = step * UNROLL + u
                if index:
                    s = listed[index, s]
                x = rows_t[pl.ds(s, STAMP, stride=stars), :]
                col = starts[index, 1, s]
                y = pltpu.roll(x, lax.rem(col, LANES), axis=1)
                placed.append((pl.ds(starts[index, 0, s] * stars + s, STAMP, stride=stars), col, y))
            for spot, col, y in placed:
                if lo is None:
                    hi[spot, :] = y
                else:
                    in_lo = lane32 >= col
                    lo[spot, :] = jnp.where(in_lo, y, 0.0)
                    hi[spot, :] = jnp.where(in_lo, 0.0, y)

    acc_top[...] = jnp.zeros_like(acc_top)
    acc_lo[...] = jnp.zeros_like(acc_lo)
    acc_hi[...] = jnp.zeros_like(acc_hi)
    row_lane = lax.broadcasted_iota(jnp.int32, (1, LANES), 1)

    def weigh(ref, y, factor):
        return (ref[pl.ds(pl.multiple_of(y * stars, stars), stars), :] * factor).astype(jnp.bfloat16)

    def group(first, rhs_sum, bottom):
        parts = {name: [] for name in ("ol", "oh", "rh", "bl", "bh", "dh")}
        some = pl.ds(pl.multiple_of(first, GROUP), GROUP)
        root_some, resid_some = root[0, some, :], resid[0, some, :]
        for u in range(GROUP):
            y = first + u
            root_lo = root_some[u:u + 1, :LANES]
            root_hi = root_some[u:u + 1, LANES:]
            root_edge = jnp.where(row_lane >= edge_lane, root_hi, 0.0)
            at = pl.ds(pl.multiple_of(y * stars, stars), stars)
            p_lo = own_lo[at, :]
            p_hi = own_hi[at, :]
            rhs_sum = rhs_sum + p_lo * resid_some[u:u + 1, :LANES] + p_hi * resid_some[u:u + 1, LANES:]
            parts["ol"].append((p_lo * root_lo).astype(jnp.bfloat16))
            parts["oh"].append((p_hi * root_hi).astype(jnp.bfloat16))
            parts["rh"].append(weigh(right_hi, y, root_edge))
            if bottom:
                parts["bl"].append(weigh(below_lo, y - tile_rows, root_lo))
                parts["bh"].append(weigh(below_hi, y - tile_rows, root_hi))
                parts["dh"].append(weigh(diag_hi, y - tile_rows, root_edge))
        q = {name: jnp.concatenate(tiles, axis=1) for name, tiles in parts.items() if tiles}
        if bottom:
            acc_lo[...] += nt_dot(q["ol"], jnp.concatenate([q["ol"], q["bl"]], axis=0))
            four = jnp.concatenate([q["oh"], q["rh"], q["bh"], q["dh"]], axis=0)
            acc_hi[...] += nt_dot(four[:2 * stars], four)
        else:
            acc_top[...] += nt_dot(q["oh"], jnp.concatenate([q["oh"], q["rh"]], axis=0))
            acc_lo[:, :stars] += nt_dot(q["ol"], q["ol"])
        return rhs_sum

    rhs_sum = jnp.zeros((stars, LANES), jnp.float32)
    rhs_sum = lax.fori_loop(0, tile_rows // GROUP, lambda g, r: group(g * GROUP, r, False), rhs_sum)
    rhs_sum = lax.fori_loop(
        0, STAMP // GROUP, lambda g, r: group(tile_rows + g * GROUP, r, True), rhs_sum
    )
    rhs[0] = jnp.sum(rhs_sum, axis=1, keepdims=True)
    n = stars
    top, low, high = acc_top[...], acc_lo[...], acc_hi[...]
    gram[0, 0] = low[:, :n] + top[:, :n] + high[:n, :n]
    gram[0, 1] = top[:, n:2 * n] + high[:n, n:2 * n]
    gram[0, 2] = low[:, n:2 * n] + high[:n, 2 * n:3 * n]
    gram[0, 3] = high[:n, 3 * n:]
    gram[0, 4] = high[n:, 2 * n:3 * n]


def compute(starts, stamp_sets, root, resid, tile_rows, tile_cols):
    bands, stars, pixels = stamp_sets[0].shape
    rows_out, cols_out = root.shape[1:]
    stamp_spec = pl.BlockSpec((1, stars, pixels), lambda b, st: (b, 0, 0))
    field_spec = pl.BlockSpec((1, rows_out, cols_out), lambda b, st: (b, 0, 0))
    tall = pltpu.VMEM((rows_out * stars, LANES), jnp.float32)
    short = pltpu.VMEM((2 * STAMP * stars, LANES), jnp.float32)

    def kernel(*refs):
        gram_kernel(*refs, stars=stars, tile_rows=tile_rows, tile_cols=tile_cols)

    return pl.pallas_call(
        kernel,
        out_shape=(
            jax.ShapeDtypeStruct((bands, 5, stars, stars), jnp.float32),
            jax.ShapeDtypeStruct((bands, stars, 1), jnp.float32),
        ),
        grid_spec=pltpu.PrefetchScalarGridSpec(
            num_scalar_prefetch=1,
            grid=(bands,),
            in_specs=[stamp_spec] * 4 + [field_spec] * 2,
            out_specs=(
                pl.BlockSpec((1, 5, stars, stars), lambda b, st: (b, 0, 0, 0)),
                pl.BlockSpec((1, stars, 1), lambda b, st: (b, 0, 0)),
            ),
            scratch_shapes=[
                pltpu.VMEM((STAMP * stars, LANES), jnp.float32),
                tall, tall, tall, short, short, short,
                pltpu.VMEM((stars, 2 * stars), jnp.float32),
                pltpu.VMEM((stars, 2 * stars), jnp.float32),
                pltpu.VMEM((2 * stars, 4 * stars), jnp.float32),
                pltpu.SMEM((4, stars + UNROLL), jnp.int32),
                pltpu.SMEM((4,), jnp.int32),
            ],
        ),
        compiler_params=pltpu.CompilerParams(vmem_limit_bytes=40 << 20),
        name="gram",
    )(starts, *stamp_sets, root, resid)


def body(stamps, positions, weights, mask, residual):
    band_count, tile_rows, tile_cols = weights.shape
    star_count = stamps.shape[3]
    half_side = STAMP // 2
    rows_out = tile_rows + STAMP
    cols_out = tile_cols + STAMP
    own, places = stamps[0, 0], positions[0, 0]
    right = shifted((own, places), "tx", -1)
    below, diag = shifted(((own, places), right), "ty", -1)

    weight = weights * mask.astype(jnp.float32)
    fields = jnp.stack((jnp.sqrt(weight), weight * residual)).astype(jnp.bfloat16)
    region = padded(fields, (("ty", 2), ("tx", 3)), half_side).astype(jnp.float32)

    anchor_row = lax.axis_index("ty") * tile_rows
    anchor_col = lax.axis_index("tx") * tile_cols

    def rows_of(pair):
        return pair[1][0] - anchor_row

    def cols_of(pair):
        return pair[1][1] - anchor_col

    mine = (own, places)
    has_right = lax.axis_index("tx") < lax.axis_size("tx") - 1
    has_below = lax.axis_index("ty") < lax.axis_size("ty") - 1

    def strip_cols(pair):
        return jnp.where(has_right, jnp.clip(cols_of(pair), tile_cols, cols_out), cols_out)

    def strip_rows(pair):
        return jnp.where(has_below, jnp.clip(rows_of(pair) - tile_rows, 0, STAMP), STAMP)

    starts = jnp.stack([
        jnp.stack([jnp.clip(rows_of(mine), 0, tile_rows), jnp.clip(cols_of(mine), 0, tile_cols)]),
        jnp.stack([jnp.clip(rows_of(right), 0, tile_rows), strip_cols(right)]),
        jnp.stack([strip_rows(below), jnp.clip(cols_of(below), 0, tile_cols)]),
        jnp.stack([strip_rows(diag), strip_cols(diag)]),
    ])
    blocks, rhs = compute(
        starts, (own, right[0], below[0], diag[0]), region[0], region[1], tile_rows, tile_cols
    )
    self_own, own_right, own_below, own_diag, right_below = [blocks[:, i] for i in range(5)]
    to_right = jnp.stack([jnp.swapaxes(own_right, 1, 2), right_below]).astype(jnp.bfloat16)
    to_below = jnp.stack([jnp.swapaxes(own_below, 1, 2), jnp.swapaxes(right_below, 1, 2)])
    from_left = shifted(to_right, "tx", 1).astype(jnp.float32)
    from_above = shifted(to_below, "ty", 1)
    corner = moved(jnp.swapaxes(own_diag, 1, 2).astype(jnp.bfloat16), 1, 1)
    gram = jnp.concatenate(
        [
            corner.astype(jnp.float32), from_above[0], from_above[1],
            from_left[0], self_own, own_right,
            from_left[1], own_below, own_diag,
        ],
        axis=2,
    )
    return (
        gram.reshape(1, 1, band_count, star_count, 9 * star_count),
        rhs.reshape(1, 1, band_count, star_count),
    )


def solution(mesh):
    return jax.shard_map(
        body,
        mesh=mesh,
        in_specs=(
            P("ty", "tx", None, None, None),
            P("ty", "tx", None, None),
            P(None, "ty", "tx"),
            P(None, "ty", "tx"),
            P(None, "ty", "tx"),
        ),
        out_specs=(P("ty", "tx", None, None, None), P("ty", "tx", None, None)),
        check_vma=False,
    )
```
